128 devices in a mesh: pipe: 8 (over x_lo, z), ctx: 16 (over y, x_hi, core).
Axes of the slice: x: 4 (x_hi: 2, x_lo: 2; x = x_hi * 2 + x_lo), y: 4, z: 4, core: 2. Of those that a mesh axis runs over, the one named last changes fastest.
Arguments:
- queries: bfloat16 [8, 6144, 4096], P('pipe', 'ctx'), may hold values from -1.796875 to 1.796875
- key_rows: bfloat16 [8, 6144, 4096], P('pipe', 'ctx'), may hold values from -1.796875 to 1.796875
- value_rows: bfloat16 [8, 6144, 4096], P('pipe', 'ctx'), may hold values from -6 to 6
- next_grads: bfloat16 [8, 6144, 4096], P('pipe', 'ctx'), may hold values from -0.29882812 to 0.29882812
- log_decay: float32 [8, 32, 6144], P('pipe', None, 'ctx'), may hold values from -1.5 to 0, as said below
- doc_ids: int32 [8, 6144], P('pipe', 'ctx'), may hold values from 0 to 3, never falling along the last dimension, each value on 1 to 3072 neighbouring positions
- prefix_states: float32 [8, 16, 32, 128, 128], P('pipe', 'ctx'), may hold values from -24 to 24
Outputs:
- grad_q: bfloat16 [8, 6144, 4096], P('pipe', 'ctx')
- grad_k: bfloat16 [8, 6144, 4096], P('pipe', 'ctx')
- grad_v: bfloat16 [8, 6144, 4096], P('pipe', 'ctx')
The draws below stay inside these ranges and needn't reach their ends.
Inputs may be any that keep to these rules, and one draw needn't show every extreme that they name: `doc_ids`: in each section ids never fall along the sequence; each of the 4 documents holds 1 to 3072 tokens, one exactly 3072. `log_decay`: every entry is negative.
All inputs are finite; a program needn't handle non-finite values.
Results may differ from the reference program's by a relative error of at most 0.0053.
Values may be sent and summed in bfloat16 or wider, within the bound.
No kernel may reach another device: no remote copies, remote signals or barrier semaphores. Data moves between devices by JAX's collectives and lax.ppermute only.
A program may use at most 192 MiB of HBM per device.

```python
import math
import jax
import jax.numpy as jnp
import numpy as np
from jax import lax

HEAD_TOTAL = 32
HEAD_DIM = 128
TOK_DEV = 384
DOCS = 4
SECTION_TOTAL = 8
SECTION_TOKENS = 6144
HD = 4096
N_CTX = 16


def draw_log_decay(key, part):
    parallel_flows = jax.random.split(key, 8)
    fast_share = 0.5
    token_factor = jnp.exp(jax.random.uniform(parallel_flows[5], (SECTION_TOTAL, HEAD_TOTAL, SECTION_TOKENS), jnp.float32, math.log(0.5), math.log(2.0)))
    fast_head = jax.random.uniform(parallel_flows[0], (SECTION_TOTAL, HEAD_TOTAL, 1), jnp.float32) < fast_share
    fast_rate = jnp.exp(jax.random.uniform(parallel_flows[1], (SECTION_TOTAL, HEAD_TOTAL, 1), jnp.float32, math.log(1.0 / 40.0), math.log(1.0 / 10.0)))
    slow_rate = jnp.exp(jax.random.uniform(parallel_flows[2], (SECTION_TOTAL, HEAD_TOTAL, 1), jnp.float32, math.log(0.05), math.log(0.4))) / SECTION_TOKENS
    base_rate = jnp.where(fast_head, fast_rate, slow_rate)
    block_factor = jnp.exp(jax.random.uniform(parallel_flows[3], (SECTION_TOTAL, HEAD_TOTAL, SECTION_TOKENS // TOK_DEV, 1), jnp.float32, math.log(0.005), math.log(2.0)))
    block_factor = jnp.broadcast_to(block_factor, (SECTION_TOTAL, HEAD_TOTAL, SECTION_TOKENS // TOK_DEV, TOK_DEV)).reshape(SECTION_TOTAL, HEAD_TOTAL, SECTION_TOKENS)
    piece_count = (SECTION_TOKENS + 63) // 64
    piece_factor = jnp.exp(jax.random.uniform(parallel_flows[7], (SECTION_TOTAL, HEAD_TOTAL, piece_count, 1), jnp.float32, math.log(0.01), math.log(3.0)))
    piece_factor = jnp.broadcast_to(piece_factor, (SECTION_TOTAL, HEAD_TOTAL, piece_count, 64)).reshape(SECTION_TOTAL, HEAD_TOTAL, piece_count * 64)[:, :, :SECTION_TOKENS]
    gentle_portion = -base_rate * block_factor * piece_factor * token_factor
    sudden_location = jax.random.randint(parallel_flows[4], (SECTION_TOTAL, 2, 1), 0, SECTION_TOKENS)
    sudden_hit = jnp.where(jnp.arange(SECTION_TOKENS)[None, None, :] == sudden_location, 1.0, 0.0)
    sudden_keep = jnp.log(jax.random.uniform(parallel_flows[6], (SECTION_TOTAL, 2, HEAD_TOTAL), jnp.float32, 0.6, 0.8))
    sudden_portion = jnp.einsum('knx,knu->kxu', sudden_keep, sudden_hit)
    return jnp.maximum(gentle_portion + sudden_portion, -1.5).astype(jnp.float32)


def shard_levels(key, dims, cuts, smallest, high):
    def one(dim, parts):
        steps = jax.random.uniform(jax.random.fold_in(jax.random.fold_in(key, 6), dim), (parts,), jnp.float32, smallest / len(cuts), high / len(cuts))
        return jnp.repeat(jnp.exp(steps), dims[dim] // parts).reshape((-1,) + (1,) * (len(dims) - dim - 1))

    gain = one(*cuts[0])
    for cut in cuts[1:]:
        gain = gain * one(*cut)
    return gain


def length_profile(amount, total, limit, lean):
    portions = [(1 << 20) // math.isqrt(standing ** lean) + 1 for standing in range(2, amount + 1)]
    spare, counts = total - limit - (amount - 1), [1] * (amount - 1)
    while spare > 0:
        movable = [i for i in range(amount - 1) if counts[i] < limit]
        mass, budget = sum([portions[i] for i in movable]), spare
        for i in movable:
            more = min(limit - counts[i], max(1, budget * portions[i] // mass), spare)
            counts[i] = counts[i] + more
            spare = spare - more
    return np.array([limit] + counts)


def ragged_sizes(key, count, total, bound, lean):
    if count == 2:
        one = jax.random.randint(key, (), max(1, total - bound), min(bound, total - 1) + 1)
        return jnp.stack([one, total - one])
    tallies = jnp.asarray(length_profile(count, total, bound, lean), jnp.int32)
    twos = (count - 1) // 2
    donor, receiver = tallies[1:1 + 2 * twos:2], tallies[2:2 + 2 * twos:2]
    margin = jnp.minimum(donor - 1, bound - receiver)
    shifted = jax.random.randint(jax.random.fold_in(key, 1), (twos,), 0, 1 << 20) % (margin + 1)
    tallies = tallies.at[1:1 + 2 * twos:2].set(donor - shifted).at[2:2 + 2 * twos:2].set(receiver + shifted)
    return tallies[jax.random.permutation(jax.random.fold_in(key, 2), count)]


def gaussian(own_key, shape, scale, limit, cuts=(), held_as=jnp.bfloat16):
    array = scale * jax.random.normal(own_key, shape, jnp.float32)
    if cuts:
        array = array * shard_levels(own_key, shape, cuts, -0.22, 0.18)
    return jnp.clip(array, -limit, limit).astype(held_as)


def setup_inputs(seed: int = 0) -> dict:
    streams_of = jax.random.split(jax.random.key(seed), 8)
    return {
        "queries": gaussian(streams_of[0], (SECTION_TOTAL, SECTION_TOKENS, HD), 0.3, 1.796875, ((0, 8), (1, 16))),
        "key_rows": gaussian(streams_of[1], (SECTION_TOTAL, SECTION_TOKENS, HD), 0.3, 1.796875, ((0, 8), (1, 16))),
        "value_rows": gaussian(streams_of[2], (SECTION_TOTAL, SECTION_TOKENS, HD), 1.0, 6.0, ((0, 8), (1, 16))),
        "next_grads": gaussian(streams_of[3], (SECTION_TOTAL, SECTION_TOKENS, HD), 0.05, 0.29882812, ((0, 8), (1, 16))),
        "log_decay": draw_log_decay(jax.random.fold_in(streams_of[7], 71), 0),
        "doc_ids": jax.vmap(lambda own: jnp.searchsorted(jnp.cumsum(ragged_sizes(own, DOCS, SECTION_TOKENS, SECTION_TOKENS // 2, 0)), jnp.arange(SECTION_TOKENS), side="right"))(jax.random.split(streams_of[5], SECTION_TOTAL)).reshape((SECTION_TOTAL, SECTION_TOKENS)).astype(jnp.int32),
        "prefix_states": gaussian(streams_of[6], (SECTION_TOTAL, N_CTX, HEAD_TOTAL, HEAD_DIM, HEAD_DIM), 4.0, 24.0, ((0, 8), (1, 16)), jnp.float32),
    }


def local_block(queries, key_rows, value_rows, grad_rows, log_decay, doc_ids, prefix_state, prior_last):
    head_count = log_decay.shape[0]
    length = queries.shape[0]
    head_dim = queries.shape[1] // head_count
    query_heads = queries.reshape(length, head_count, head_dim).astype(jnp.float32)
    key_heads = key_rows.reshape(length, head_count, head_dim).astype(jnp.float32)
    value_heads = value_rows.reshape(length, head_count, head_dim).astype(jnp.float32)
    grad_heads = grad_rows.reshape(length, head_count, head_dim).astype(jnp.float32)
    running = jnp.cumsum(log_decay, axis=1)
    block_total = running[:, -1]
    position = jnp.arange(length)
    same_doc = (doc_ids[:, None] == doc_ids[None, :]) & (position[None, :] <= position[:, None])
    spread = running[:, :, None] - running[:, None, :]
    weight = jnp.where(same_doc[None], jnp.exp(jnp.where(same_doc[None], spread, 0.0)), 0.0)
    scores = jnp.einsum("ihd,jhd->hij", query_heads, key_heads)
    attention = lax.optimization_barrier((weight * scores).astype(jnp.bfloat16)).astype(jnp.float32)
    grad_dots = jnp.einsum("ihd,jhd->hij", grad_heads, value_heads)
    grad_mix = lax.optimization_barrier((weight * grad_dots).astype(jnp.bfloat16)).astype(jnp.float32)
    continues = prior_last == doc_ids[0] + 1
    head_mask = jnp.where((doc_ids == doc_ids[0]) & continues, 1.0, 0.0)
    head_weight = jnp.exp(running).T * head_mask[:, None]
    weighted = lax.optimization_barrier((head_weight[:, :, None] * grad_heads).astype(jnp.bfloat16)).astype(jnp.float32)
    head_state = jnp.einsum("ihd,ihe->hde", query_heads, weighted)
    carry_link = jnp.where((doc_ids[0] == doc_ids[-1]) & continues, jnp.exp(block_total), 0.0)
    prefix_low = lax.optimization_barrier(prefix_state.astype(jnp.bfloat16)).astype(jnp.float32)
    grad_prefix = jnp.einsum("hde,ihe->ihd", prefix_low, grad_heads) * head_weight[:, :, None]
    grad_query = (jnp.einsum("hij,jhd->ihd", grad_mix, key_heads) + grad_prefix).astype(jnp.bfloat16)
    key_inner = jnp.einsum("hij,ihd->jhd", grad_mix, query_heads)
    value_inner = jnp.einsum("hij,ihd->jhd", attention, grad_heads)
    tail_mask = (doc_ids == doc_ids[-1])[None, :]
    tail_weight = jnp.where(tail_mask, jnp.exp(jnp.where(tail_mask, block_total[:, None] - running, 0.0)), 0.0).T
    return grad_query.reshape(length, -1), key_inner, value_inner, head_state, carry_link, tail_weight


def finish_block(key_inner, value_inner, suffix, tail_weight, key_rows, value_rows):
    length = key_rows.shape[0]
    head_count = suffix.shape[0]
    head_dim = suffix.shape[1]
    key_heads = key_rows.reshape(length, head_count, head_dim).astype(jnp.float32)
    value_heads = value_rows.reshape(length, head_count, head_dim).astype(jnp.float32)
    suffix_low = lax.optimization_barrier(suffix.astype(jnp.bfloat16)).astype(jnp.float32)
    grad_key = key_inner + jnp.einsum("hde,jhe->jhd", suffix_low, value_heads) * tail_weight[:, :, None]
    grad_value = value_inner + jnp.einsum("hde,jhd->jhe", suffix_low, key_heads) * tail_weight[:, :, None]
    return grad_key.astype(jnp.bfloat16).reshape(length, -1), grad_value.astype(jnp.bfloat16).reshape(length, -1)


def reference(queries, key_rows, value_rows, next_grads, log_decay, doc_ids, prefix_states):
    query_list, key_list, value_list = [], [], []
    for section in range(SECTION_TOTAL):
        out_grads = next_grads[(section + 1) % SECTION_TOTAL]
        doc_row = doc_ids[section]
        block_last = doc_row[TOK_DEV - 1::TOK_DEV]
        prior = jnp.concatenate([jnp.zeros((1,), jnp.int32), (block_last[:-1] + 1).astype(jnp.int32)])
        width = queries.shape[2]
        heads_here = log_decay.shape[1]
        query_blocks = queries[section].reshape(N_CTX, TOK_DEV, width)
        key_blocks = key_rows[section].reshape(N_CTX, TOK_DEV, width)
        value_blocks = value_rows[section].reshape(N_CTX, TOK_DEV, width)
        grad_blocks = out_grads.reshape(N_CTX, TOK_DEV, width)
        decay_blocks = jnp.transpose(log_decay[section].reshape(heads_here, N_CTX, TOK_DEV), (1, 0, 2))
        doc_blocks = doc_row.reshape(N_CTX, TOK_DEV)

        def run_local(packed):
            return local_block(*packed)

        grad_query, key_inner, value_inner, head_state, carry_link, tail_weight = lax.map(
            run_local, (query_blocks, key_blocks, value_blocks, grad_blocks, decay_blocks, doc_blocks,
                        prefix_states[section], prior))

        def chain_step(carry_state, element):
            link_now, state_now = element
            return state_now + link_now[:, None, None] * carry_state, carry_state

        final_state, suffix = lax.scan(chain_step, jnp.zeros_like(head_state[0]), (carry_link, head_state), reverse=True)

        def run_finish(packed):
            return finish_block(*packed)

        grad_key, grad_value = lax.map(run_finish, (key_inner, value_inner, suffix, tail_weight, key_blocks, value_blocks))
        query_list.append(grad_query.reshape(SECTION_TOKENS, width))
        key_list.append(grad_key.reshape(SECTION_TOKENS, width))
        value_list.append(grad_value.reshape(SECTION_TOKENS, width))
    return jnp.stack(query_list), jnp.stack(key_list), jnp.stack(value_list)
```

```python
import functools

import jax
import jax.numpy as jnp
from jax import lax
from jax.experimental import pallas as pl
from jax.experimental.pallas import tpu as pltpu
from jax.sharding import PartitionSpec as P

D = 128
GROUPS = ((12, 12), (4, 4))
CHUNKS = sum(GROUPS, ())
PAIR = 2
PACK = 8
VMEM_BYTES = 36 << 20
NT = (((1,), (1,)), ((), ()))
NN = (((1,), (0,)), ((), ()))
TN = (((0,), (0,)), ((), ()))


def dot(a, b, dims):
    return lax.dot_general(a, b, dims, preferred_element_type=jnp.float32)


def lane(columns, n):
    return jnp.broadcast_to(columns[:, n : n + 1], (columns.shape[0], D))


def state_of(q, g, head_weight):
    weighted = (head_weight * g.astype(jnp.float32)).astype(jnp.bfloat16)
    return dot(q, weighted, TN)


def state_kernel(side_ref, q_ref, g_ref, pack_ref, state_ref):
    columns = jnp.transpose(pack_ref[0])
    for a in range(PAIR):
        cols = slice(a * D, (a + 1) * D)
        state_ref[a] = state_of(q_ref[0, :, cols], g_ref[0, :, cols], lane(columns, PAIR + a))


class Place:
    def __init__(self, start, heads, length, other_first, skipped=0):
        self.steps = heads // PAIR
        half = self.steps // 2
        base = start // PAIR
        width = PAIR * D

        def place(t, side):
            early = 1 - side[0] if other_first else side[0]
            return jnp.where(t < half, early * half + t, (1 - early) * half + t - half)

        skip = skipped // PAIR
        self.mine = pl.BlockSpec((PAIR, D, D), lambda t, s: (skip + jnp.minimum(t, half - 1), 0, 0))
        self.other = pl.BlockSpec((PAIR, D, D), lambda t, s: (skip + jnp.maximum(t - half, 0), 0, 0))
        self.state = pl.BlockSpec((PAIR, D, D), lambda t, s: (t, 0, 0))
        self.wide = pl.BlockSpec((1, length, width), lambda t, s: (0, 0, base + place(t, s)))
        self.chunk = pl.BlockSpec((1, length, width), lambda t, s: (0, 0, place(t, s)))
        self.flat = pl.BlockSpec((length, width), lambda t, s: (0, place(t, s)))
        self.square = pl.BlockSpec((1, 1, PAIR, D, D), lambda t, s: (0, 0, base + place(t, s), 0, 0))
        self.pack = pl.BlockSpec((1, PACK, length), lambda t, s: (base + place(t, s), 0, 0))
        self.whole = pl.BlockSpec((length, length), lambda t, s: (0, 0))


def call(kernel, name, place, side, args, specs, out_shapes, out_specs, kept, cost):
    args = [side, *args]
    specs = list(specs)
    aliases = {}
    for n, value in enumerate(kept):
        if value is not None:
            aliases[len(args)] = n
            args.append(value)
            specs.append(pl.BlockSpec(memory_space=pl.ANY))
    return pl.pallas_call(
        kernel,
        out_shape=tuple(out_shapes),
        grid_spec=pltpu.PrefetchScalarGridSpec(
            num_scalar_prefetch=1, grid=(place.steps,), in_specs=specs, out_specs=list(out_specs)
        ),
        input_output_aliases=aliases,
        compiler_params=pltpu.CompilerParams(vmem_limit_bytes=VMEM_BYTES),
        cost_estimate=pl.CostEstimate(**cost),
        name=name,
    )(*args)


def states_of(side, q, g, pack, start, heads):
    length = q.shape[1]
    at = Place(start, heads, length, True)
    state = jax.ShapeDtypeStruct((heads, D, D), jnp.float32)
    cost = dict(
        flops=heads * length * D * D * 2, bytes_accessed=heads * length * D * 4, transcendentals=0
    )
    return call(
        state_kernel,
        "head_states",
        at,
        side,
        (q, g, pack),
        (at.wide, at.chunk, at.pack),
        (state,),
        (at.state,),
        (),
        cost,
    )[0]


def inner_kernel(with_states, side_ref, q_ref, k_ref, v_ref, g_ref, p_ref, mask_ref, pack_ref, *rest):
    if with_states:
        gq_ref, gk_ref, gv_ref, state_ref = rest[-4:]
    else:
        gq_ref, gk_ref, gv_ref = rest[-3:]
    length = q_ref.shape[1]
    blocks = length // D
    columns = jnp.transpose(pack_ref[0])
    for a in range(PAIR):
        cols = slice(a * D, (a + 1) * D)
        q = q_ref[0, :, cols]
        k = k_ref[0, :, cols]
        v = v_ref[0, :, cols]
        g = g_ref[0, :, cols]
        head_weight = lane(columns, PAIR + a)
        if with_states:
            state_ref[a] = state_of(q, g, head_weight)
        row = pack_ref[0, a : a + 1, :]
        col = lane(columns, a)
        mixes = []
        for j in range(blocks):
            js = slice(j * D, (j + 1) * D)
            width = length - j * D
            late = slice(j * D, length)
            spread = row[:, late] - jnp.concatenate([col[js]] * (width // D), axis=1)
            weight = jnp.exp(spread + mask_ref[js, late])
            attention = (weight * dot(k[js], q[late], NT)).astype(jnp.bfloat16)
            mix = (weight * dot(v[js], g[late], NT)).astype(jnp.bfloat16)
            mixes.append(mix)
            gv_ref[js, cols] = dot(attention, g[late], NN)
            gk_ref[js, cols] = dot(mix, q[late], NN)
        prefix = dot(g, p_ref[0, 0, a].astype(jnp.bfloat16), NT) * head_weight
        for i in range(blocks):
            rows = slice(i * D, (i + 1) * D)
            parts = [mixes[j][:, (i - j) * D : (i - j + 1) * D] for j in range(i + 1)]
            mix = parts[0] if i == 0 else jnp.concatenate(parts, axis=0)
            gq = dot(mix, k[: (i + 1) * D], TN) + prefix[rows]
            gq_ref[0, rows, cols] = gq.astype(gq_ref.dtype)


def inner_of(side, q, k, v, g, prefix, mask, pack, out, start, heads, with_states):
    length = q.shape[1]
    at = Place(start, heads, length, True)
    partial = jax.ShapeDtypeStruct((length, heads * D), jnp.float32)
    state = jax.ShapeDtypeStruct((heads, D, D), jnp.float32)
    whole = jax.ShapeDtypeStruct(q.shape, jnp.bfloat16)
    cost = dict(
        flops=heads * 33 * 2 * D * D * D,
        bytes_accessed=heads * length * D * 18,
        transcendentals=heads * length * length // 2,
    )
    return call(
        functools.partial(inner_kernel, with_states),
        "inner_grads",
        at,
        side,
        (q, k, v, g, prefix, mask, pack),
        (at.wide, at.wide, at.wide, at.chunk, at.square, at.whole, at.pack),
        (whole, partial, partial) + ((state,) if with_states else ()),
        (at.wide, at.flat, at.flat) + ((at.state,) if with_states else ()),
        (out,),
        cost,
    )


def finish_kernel(side_ref, k_ref, v_ref, ki_ref, vi_ref, mine_ref, other_ref, pack_ref, *rest):
    gk_ref, gv_ref = rest[-2:]
    first = pl.program_id(0) < pl.num_programs(0) // 2
    columns = jnp.transpose(pack_ref[0])
    for a in range(PAIR):
        cols = slice(a * D, (a + 1) * D)
        weight = lane(columns, 2 * PAIR + a)
        suffix = jnp.where(first, mine_ref[a], other_ref[a])
        gk = ki_ref[:, cols] + weight * dot(v_ref[0, :, cols], suffix, NT)
        gv = vi_ref[:, cols] + weight * dot(k_ref[0, :, cols], suffix, NN)
        gk_ref[0, :, cols] = gk.astype(gk_ref.dtype)
        gv_ref[0, :, cols] = gv.astype(gv_ref.dtype)


def finish_of(side, k, v, key_inner, value_inner, mine, other, pack, outs, start, heads, skipped):
    length = k.shape[1]
    at = Place(start, heads, length, False, skipped)
    whole = jax.ShapeDtypeStruct(k.shape, jnp.bfloat16)
    cost = dict(
        flops=heads * 6 * 2 * D * D * D, bytes_accessed=heads * length * D * 16, transcendentals=0
    )
    return call(
        finish_kernel,
        "finish_grads",
        at,
        side,
        (k, v, key_inner, value_inner, mine, other, pack),
        (at.wide, at.wide, at.flat, at.flat, at.mine, at.other, at.pack),
        (whole, whole),
        (at.wide, at.wide),
        outs,
        cost,
    )


def moved(value, pairs):
    return lax.ppermute(value, "ctx", pairs)


def part_of(table, first, count):
    return lax.dynamic_slice_in_dim(table, first, count)[:, None, None]


def after(value, *others):
    return lax.optimization_barrier((value, *others))[0]


def on_device(queries, key_rows, value_rows, next_grads, log_decay, doc_ids, prefix_states):
    pipe = lax.axis_size("pipe")
    ctx = lax.axis_size("ctx")
    length = queries.shape[1]
    back = [((i + 1) % pipe, i) for i in range(pipe)]
    core_swap = [(i, i ^ 1) for i in range(ctx)]
    chip_swap = [(i, i ^ 2) for i in range(ctx)]
    row_up = [[(i, i - 4 * d) for i in range(4 * d, ctx)] for d in (1, 2)]

    starts = [sum(CHUNKS[:n]) for n in range(len(CHUNKS))]
    docs = doc_ids[0]
    prior = lax.ppermute(docs[-1:] + 1, "ctx", [(i, i + 1) for i in range(ctx - 1)])[0]
    place = lax.axis_index("ctx")
    side = place % 2
    pair = (place // 2) % 2
    even = side == 0
    near = pair == 0
    continues = prior == docs[0] + 1
    position = lax.iota(jnp.int32, length)
    upto = jnp.where(position[:, None] <= position[None, :], 1.0, 0.0)
    running = jnp.dot(log_decay[0], upto, precision=lax.Precision.HIGHEST)
    allowed = (docs[:, None] == docs[None, :]) & (position[:, None] <= position[None, :])
    mask = jnp.where(allowed, 0.0, -1e30)
    total = running[:, -1:]
    head_weight = jnp.exp(running) * jnp.where((docs == docs[0]) & continues, 1.0, 0.0)
    tail_weight = jnp.exp(total - running) * jnp.where(docs == docs[-1], 1.0, 0.0)
    pack = jnp.concatenate(
        [
            value.reshape(-1, PAIR, length)
            for value in (running, head_weight, tail_weight, jnp.zeros_like(running))
        ],
        axis=1,
    )
    link = jnp.where((docs[0] == docs[-1]) & continues, jnp.exp(running[:, -1]), 0.0)
    partner = moved(link, core_swap)
    link_even = jnp.where(even, link, partner)
    link_odd = jnp.where(even, partner, link)
    chip_link = link_even * link_odd
    near_table = jnp.stack([chip_link] + [moved(chip_link, pairs) for pairs in row_up])
    side_arr = side.astype(jnp.int32).reshape(1)

    grads = []
    for n, (start, size) in enumerate(zip(starts, CHUNKS)):
        ready = (prior, chip_link, near_table, grads[0] if n else None)[min(n, 3)]
        part = lax.slice_in_dim(after(next_grads, ready), start * D, (start + size) * D, axis=2)
        grads.append(lax.ppermute(part, "pipe", back))

    def halves(table, members):
        return jnp.concatenate([part_of(table, starts[n] + side * (CHUNKS[n] // 2), CHUNKS[n] // 2) for n in members])

    held = []
    out = None
    members = []
    for group in GROUPS:
        begin = members[-1] + 1 if members else 0
        members = list(range(begin, begin + len(group)))
        inner = {}
        states = []
        late = None
        for n in members:
            start, size, grad = starts[n], CHUNKS[n], grads[n]
            if out is not None:
                grad = after(grad, out)
            inputs = (prefix_states, mask, pack, out, start, size)
            if n == len(CHUNKS) - 1:
                state = states_of(side_arr, queries, grad, pack, start, size)
                late = (n, grad, inputs)
            else:
                out, *inner[n], state = inner_of(side_arr, queries, key_rows, value_rows, grad, *inputs, True)
            states.append(state)
        other = jnp.concatenate([state[: state.shape[0] // 2] for state in states])
        mine = jnp.concatenate([state[state.shape[0] // 2 :] for state in states])
        came = moved(other, core_swap)
        even_state = jnp.where(even, mine, came)
        odd_state = jnp.where(even, came, mine)
        state = even_state + halves(link_even, members) * odd_state
        low = state.astype(jnp.bfloat16)
        later = [moved(low, pairs) for pairs in row_up]
        if late is not None:
            n, grad, inputs = late
            out, *inner[n] = inner_of(side_arr, queries, key_rows, value_rows, after(grad, low), *inputs, False)
        held.append((members, odd_state, state, later, inner))

    beside = after(moved(near_table, chip_swap), held[-1][2])
    near_rows = jnp.where(near, near_table, beside)
    far_rows = jnp.where(near, beside, near_table)
    far_link, next_near, next_far, last_near = far_rows[0], near_rows[1], far_rows[1], near_rows[2]
    own_coef = [
        jnp.where(near, far_link, next_near),
        jnp.where(near, far_link * next_near * next_far, next_near * next_far * last_near),
    ]
    sent_coef = jnp.where(near, next_near * next_far, far_link * next_near)
    outs = (None, None)
    for members, odd_state, state, later, inner in held:
        if members[-1] < len(CHUNKS) - 1:
            state = after(state, grads[-1])
        later = [value.astype(jnp.float32) for value in later]
        near_coef, far_coef = (halves(table, members) for table in own_coef)
        coef = halves(sent_coef, members)
        sent = jnp.where(near, later[0] + coef * later[1], state + coef * later[0])
        came = moved(sent.astype(jnp.bfloat16), chip_swap).astype(jnp.float32)
        suffix = near_coef * later[0] + far_coef * later[1] + came
        within = odd_state + halves(link_odd, members) * suffix
        mine_suffix = jnp.where(even, within, suffix).astype(jnp.bfloat16)
        send_suffix = jnp.where(even, suffix, within).astype(jnp.bfloat16)
        other_suffix = moved(send_suffix, core_swap)
        skipped = 0
        for n in members:
            outs = finish_of(
                side_arr,
                key_rows,
                value_rows,
                *inner[n],
                mine_suffix,
                other_suffix,
                pack,
                outs,
                starts[n],
                CHUNKS[n],
                skipped,
            )
            skipped += CHUNKS[n] // 2
    return (out, *outs)


def solution(mesh):
    rows = P("pipe", "ctx", None)
    return jax.shard_map(
        on_device,
        mesh=mesh,
        in_specs=(
            rows,
            rows,
            rows,
            rows,
            P("pipe", None, "ctx"),
            P("pipe", "ctx"),
            P("pipe", "ctx", None, None, None),
        ),
        out_specs=(rows, rows, rows),
        check_vma=False,
    )
```

```python
import functools

import jax
import jax.numpy as jnp
from jax import lax
from jax.experimental import pallas as pl
from jax.experimental.pallas import tpu as pltpu
from jax.sharding import PartitionSpec as P

D = 128
GROUPS = ((8, 12), (8, 4))
CHUNKS = sum(GROUPS, ())
PAIR = 2
PACK = 8
VMEM_BYTES = 36 << 20
NT = (((1,), (1,)), ((), ()))
NN = (((1,), (0,)), ((), ()))
TN = (((0,), (0,)), ((), ()))


def dot(a, b, dims):
    return lax.dot_general(a, b, dims, preferred_element_type=jnp.float32)


def lane(columns, n):
    return jnp.broadcast_to(columns[:, n : n + 1], (columns.shape[0], D))


def state_of(q, g, head_weight):
    weighted = (head_weight * g.astype(jnp.float32)).astype(jnp.bfloat16)
    return dot(q, weighted, TN)


def state_kernel(side_ref, q_ref, g_ref, pack_ref, state_ref):
    columns = jnp.transpose(pack_ref[0])
    for a in range(PAIR):
        cols = slice(a * D, (a + 1) * D)
        state_ref[a] = state_of(q_ref[0, :, cols], g_ref[0, :, cols], lane(columns, PAIR + a))


class Place:
    def __init__(self, start, heads, length, other_first, skipped=0):
        self.steps = heads // PAIR
        half = self.steps // 2
        base = start // PAIR
        width = PAIR * D

        def place(t, side):
            early = 1 - side[0] if other_first else side[0]
            return jnp.where(t < half, early * half + t, (1 - early) * half + t - half)

        skip = skipped // PAIR
        self.mine = pl.BlockSpec((PAIR, D, D), lambda t, s: (skip + jnp.minimum(t, half - 1), 0, 0))
        self.other = pl.BlockSpec((PAIR, D, D), lambda t, s: (skip + jnp.maximum(t - half, 0), 0, 0))
        self.state = pl.BlockSpec((PAIR, D, D), lambda t, s: (t, 0, 0))
        self.wide = pl.BlockSpec((1, length, width), lambda t, s: (0, 0, base + place(t, s)))
        self.chunk = pl.BlockSpec((1, length, width), lambda t, s: (0, 0, place(t, s)))
        self.flat = pl.BlockSpec((length, width), lambda t, s: (0, place(t, s)))
        self.square = pl.BlockSpec((1, 1, PAIR, D, D), lambda t, s: (0, 0, base + place(t, s), 0, 0))
        self.pack = pl.BlockSpec((1, PACK, length), lambda t, s: (base + place(t, s), 0, 0))
        self.whole = pl.BlockSpec((length, length), lambda t, s: (0, 0))


def call(kernel, name, place, side, args, specs, out_shapes, out_specs, kept, cost, limit=VMEM_BYTES):
    args = [side, *args]
    specs = list(specs)
    aliases = {}
    for n, value in enumerate(kept):
        if value is not None:
            aliases[len(args)] = n
            args.append(value)
            specs.append(pl.BlockSpec(memory_space=pl.ANY))
    return pl.pallas_call(
        kernel,
        out_shape=tuple(out_shapes),
        grid_spec=pltpu.PrefetchScalarGridSpec(
            num_scalar_prefetch=1, grid=(place.steps,), in_specs=specs, out_specs=list(out_specs)
        ),
        input_output_aliases=aliases,
        compiler_params=pltpu.CompilerParams(vmem_limit_bytes=limit),
        cost_estimate=pl.CostEstimate(**cost),
        name=name,
    )(*args)


def states_of(side, q, g, pack, start, heads):
    length = q.shape[1]
    at = Place(start, heads, length, True)
    state = jax.ShapeDtypeStruct((heads, D, D), jnp.float32)
    cost = dict(
        flops=heads * length * D * D * 2, bytes_accessed=heads * length * D * 26, transcendentals=0
    )
    return call(
        state_kernel,
        "head_states",
        at,
        side,
        (q, g, pack),
        (at.wide, at.chunk, at.pack),
        (state,),
        (at.state,),
        (),
        cost,
    )[0]


def inner_kernel(with_states, side_ref, q_ref, k_ref, v_ref, g_ref, p_ref, mask_ref, pack_ref, *rest):
    if with_states:
        gq_ref, gk_ref, gv_ref, state_ref = rest[-4:]
    else:
        gq_ref, gk_ref, gv_ref = rest[-3:]
    length = q_ref.shape[1]
    blocks = length // D
    columns = jnp.transpose(pack_ref[0])
    for a in range(PAIR):
        cols = slice(a * D, (a + 1) * D)
        q = q_ref[0, :, cols]
        k = k_ref[0, :, cols]
        v = v_ref[0, :, cols]
        g = g_ref[0, :, cols]
        head_weight = lane(columns, PAIR + a)
        if with_states:
            state_ref[a] = state_of(q, g, head_weight)
        row = pack_ref[0, a : a + 1, :]
        col = lane(columns, a)
        mixes = []
        for j in range(blocks):
            js = slice(j * D, (j + 1) * D)
            width = length - j * D
            late = slice(j * D, length)
            spread = row[:, late] - jnp.concatenate([col[js]] * (width // D), axis=1)
            weight = jnp.exp(spread + mask_ref[js, late])
            attention = (weight * dot(k[js], q[late], NT)).astype(jnp.bfloat16)
            mix = (weight * dot(v[js], g[late], NT)).astype(jnp.bfloat16)
            mixes.append(mix)
            gv_ref[js, cols] = dot(attention, g[late], NN)
            gk_ref[js, cols] = dot(mix, q[late], NN)
        prefix = dot(g, p_ref[0, 0, a].astype(jnp.bfloat16), NT) * head_weight
        for i in range(blocks):
            rows = slice(i * D, (i + 1) * D)
            parts = [mixes[j][:, (i - j) * D : (i - j + 1) * D] for j in range(i + 1)]
            mix = parts[0] if i == 0 else jnp.concatenate(parts, axis=0)
            gq = dot(mix, k[: (i + 1) * D], TN) + prefix[rows]
            gq_ref[0, rows, cols] = gq.astype(gq_ref.dtype)


def inner_of(side, q, k, v, g, prefix, mask, pack, out, start, heads, with_states):
    length = q.shape[1]
    at = Place(start, heads, length, True)
    partial = jax.ShapeDtypeStruct((length, heads * D), jnp.float32)
    state = jax.ShapeDtypeStruct((heads, D, D), jnp.float32)
    whole = jax.ShapeDtypeStruct(q.shape, jnp.bfloat16)
    cost = dict(
        flops=heads * 33 * 2 * D * D * D,
        bytes_accessed=heads * length * D * 80,
        transcendentals=heads * length * length // 2,
    )
    return call(
        functools.partial(inner_kernel, with_states),
        "inner_grads",
        at,
        side,
        (q, k, v, g, prefix, mask, pack),
        (at.wide, at.wide, at.wide, at.chunk, at.square, at.whole, at.pack),
        (whole, partial, partial) + ((state,) if with_states else ()),
        (at.wide, at.flat, at.flat) + ((at.state,) if with_states else ()),
        (out,),
        cost,
        VMEM_BYTES if start else 58 << 20,
    )


def finish_kernel(side_ref, k_ref, v_ref, ki_ref, vi_ref, mine_ref, other_ref, pack_ref, *rest):
    gk_ref, gv_ref = rest[-2:]
    first = pl.program_id(0) < pl.num_programs(0) // 2
    columns = jnp.transpose(pack_ref[0])
    for a in range(PAIR):
        cols = slice(a * D, (a + 1) * D)
        weight = lane(columns, 2 * PAIR + a)
        suffix = jnp.where(first, mine_ref[a], other_ref[a])
        gk = ki_ref[:, cols] + weight * dot(v_ref[0, :, cols], suffix, NT)
        gv = vi_ref[:, cols] + weight * dot(k_ref[0, :, cols], suffix, NN)
        gk_ref[0, :, cols] = gk.astype(gk_ref.dtype)
        gv_ref[0, :, cols] = gv.astype(gv_ref.dtype)


def finish_of(side, k, v, key_inner, value_inner, mine, other, pack, outs, start, heads, skipped):
    length = k.shape[1]
    at = Place(start, heads, length, False, skipped)
    whole = jax.ShapeDtypeStruct(k.shape, jnp.bfloat16)
    cost = dict(
        flops=heads * 6 * 2 * D * D * D, bytes_accessed=heads * length * D * 30, transcendentals=0
    )
    return call(
        finish_kernel,
        "finish_grads",
        at,
        side,
        (k, v, key_inner, value_inner, mine, other, pack),
        (at.wide, at.wide, at.flat, at.flat, at.mine, at.other, at.pack),
        (whole, whole),
        (at.wide, at.wide),
        outs,
        cost,
    )


def moved(value, pairs):
    return lax.ppermute(value, "ctx", pairs)


def part_of(table, first, count):
    return lax.dynamic_slice_in_dim(table, first, count)[:, None, None]


def after(value, *others):
    return lax.optimization_barrier((value, *others))[0]


def on_device(queries, key_rows, value_rows, next_grads, log_decay, doc_ids, prefix_states):
    pipe = lax.axis_size("pipe")
    ctx = lax.axis_size("ctx")
    length = queries.shape[1]
    back = [((i + 1) % pipe, i) for i in range(pipe)]
    core_swap = [(i, i ^ 1) for i in range(ctx)]
    chip_swap = [(i, i ^ 2) for i in range(ctx)]
    row_up = [[(i, i - 4 * d) for i in range(4 * d, ctx)] for d in (1, 2)]

    starts = [sum(CHUNKS[:n]) for n in range(len(CHUNKS))]
    docs = doc_ids[0]
    opening = lax.slice_in_dim(next_grads, 0, CHUNKS[0] * D, axis=2)
    grads = [lax.ppermute(opening, "pipe", back)]
    docs, log_decay = lax.optimization_barrier((docs, log_decay, opening))[:2]
    prior = lax.ppermute(docs[-1:] + 1, "ctx", [(i, i + 1) for i in range(ctx - 1)])[0]

    place = lax.axis_index("ctx")
    side = place % 2
    pair = (place // 2) % 2
    even = side == 0
    near = pair == 0
    continues = prior == docs[0] + 1
    position = lax.iota(jnp.int32, length)
    upto = jnp.where(position[:, None] <= position[None, :], 1.0, 0.0)
    running = jnp.dot(log_decay[0], upto, precision=lax.Precision.HIGHEST)
    allowed = (docs[:, None] == docs[None, :]) & (position[:, None] <= position[None, :])
    mask = jnp.where(allowed, 0.0, -1e30)
    total = running[:, -1:]
    head_weight = jnp.exp(running) * jnp.where((docs == docs[0]) & continues, 1.0, 0.0)
    tail_weight = jnp.exp(total - running) * jnp.where(docs == docs[-1], 1.0, 0.0)
    pack = jnp.concatenate(
        [
            value.reshape(-1, PAIR, length)
            for value in (running, head_weight, tail_weight, jnp.zeros_like(running))
        ],
        axis=1,
    )
    link = jnp.where((docs[0] == docs[-1]) & continues, jnp.exp(running[:, -1]), 0.0)
    side_arr = side.astype(jnp.int32).reshape(1)

    for start, size in list(zip(starts, CHUNKS))[1:]:
        part = lax.slice_in_dim(after(next_grads, running), start * D, (start + size) * D, axis=2)
        grads.append(lax.ppermute(after(part, grads[0]), "pipe", back))

    def halves(table, members):
        return jnp.concatenate([part_of(table, starts[n] + side * (CHUNKS[n] // 2), CHUNKS[n] // 2) for n in members])

    held = []
    out = None
    members = []
    for group in GROUPS:
        begin = members[-1] + 1 if members else 0
        members = list(range(begin, begin + len(group)))
        inner = {}
        states = []
        late = None
        for n in members:
            start, size, grad = starts[n], CHUNKS[n], grads[n]
            if out is not None:
                grad = after(grad, out)
            if begin and n < len(CHUNKS) - 1:
                grad = after(grad, low)
            inputs = (prefix_states, mask, pack, out, start, size)
            if n == len(CHUNKS) - 1:
                state = states_of(side_arr, queries, grad, pack, start, size)
                late = (n, grad, inputs)
                before_last = out
            else:
                out, *inner[n], state = inner_of(side_arr, queries, key_rows, value_rows, grad, *inputs, True)
            states.append(state)
            if n == 0:
                first_out = out
        if begin == 0:
            link = after(link, first_out)
            partner = moved(link, core_swap)
            link_even = jnp.where(even, link, partner)
            link_odd = jnp.where(even, partner, link)
            chip_link = link_even * link_odd
            near_table = jnp.stack([chip_link] + [moved(chip_link, pairs) for pairs in row_up])
        other = jnp.concatenate([state[: state.shape[0] // 2] for state in states])
        mine = jnp.concatenate([state[state.shape[0] // 2 :] for state in states])
        came = moved(other, core_swap)
        if begin:
            came = after(came, *held[-1][3])
        even_state = jnp.where(even, mine, came)
        odd_state = jnp.where(even, came, mine)
        state = even_state + halves(link_even, members) * odd_state
        low = state.astype(jnp.bfloat16)
        later = [moved(low, pairs) for pairs in row_up]
        if late is not None:
            n, grad, inputs = late
            out, *inner[n] = inner_of(side_arr, queries, key_rows, value_rows, after(grad, low), *inputs, False)
        held.append((members, odd_state, state, later, inner))

    beside = after(moved(near_table, chip_swap), before_last)
    near_rows = jnp.where(near, near_table, beside)
    far_rows = jnp.where(near, beside, near_table)
    far_link, next_near, next_far, last_near = far_rows[0], near_rows[1], far_rows[1], near_rows[2]
    own_coef = [
        jnp.where(near, far_link, next_near),
        jnp.where(near, far_link * next_near * next_far, next_near * next_far * last_near),
    ]
    sent_coef = jnp.where(near, next_near * next_far, far_link * next_near)
    outs = (None, None)
    for members, odd_state, state, later, inner in held:
        state = after(state, out if members[-1] == len(CHUNKS) - 1 else grads[-1])
        later = [value.astype(jnp.float32) for value in later]
        near_coef, far_coef = (halves(table, members) for table in own_coef)
        coef = halves(sent_coef, members)
        sent = jnp.where(near, later[0] + coef * later[1], state + coef * later[0])
        came = moved(sent.astype(jnp.bfloat16), chip_swap)
        came = after(came, out) if outs[0] is None else after(came, *first_outs)
        came = came.astype(jnp.float32)
        suffix = near_coef * later[0] + far_coef * later[1] + came
        within = odd_state + halves(link_odd, members) * suffix
        mine_suffix = jnp.where(even, within, suffix).astype(jnp.bfloat16)
        send_suffix = jnp.where(even, suffix, within).astype(jnp.bfloat16)
        other_suffix = moved(send_suffix, core_swap)
        skipped = 0
        for n in members:
            outs = finish_of(
                side_arr,
                key_rows,
                value_rows,
                *inner[n],
                mine_suffix,
                other_suffix,
                pack,
                outs,
                starts[n],
                CHUNKS[n],
                skipped,
            )
            skipped += CHUNKS[n] // 2
            if n == 0:
                first_outs = outs
    return (out, *outs)


def solution(mesh):
    rows = P("pipe", "ctx", None)
    return jax.shard_map(
        on_device,
        mesh=mesh,
        in_specs=(
            rows,
            rows,
            rows,
            rows,
            P("pipe", None, "ctx"),
            P("pipe", "ctx"),
            P("pipe", "ctx", None, None, None),
        ),
        out_specs=(rows, rows, rows),
        check_vma=False,
    )
```

```python
import functools

import jax
import jax.numpy as jnp
from jax import lax
from jax.experimental import pallas as pl
from jax.experimental.pallas import tpu as pltpu
from jax.sharding import PartitionSpec as P

D = 128
GROUPS = ((8, 12), (8, 4))
CHUNKS = sum(GROUPS, ())
PAIR = 2
PACK = 8
VMEM_BYTES = 36 << 20
NT = (((1,), (1,)), ((), ()))
NN = (((1,), (0,)), ((), ()))
TN = (((0,), (0,)), ((), ()))


def dot(a, b, dims):
    return lax.dot_general(a, b, dims, preferred_element_type=jnp.float32)


def lane(columns, n):
    return jnp.broadcast_to(columns[:, n : n + 1], (columns.shape[0], D))


def state_of(q, g, head_weight):
    weighted = (head_weight * g.astype(jnp.float32)).astype(jnp.bfloat16)
    return dot(q, weighted, TN)


def state_kernel(side_ref, q_ref, g_ref, pack_ref, state_ref):
    columns = jnp.transpose(pack_ref[0])
    for a in range(PAIR):
        cols = slice(a * D, (a + 1) * D)
        state_ref[a] = state_of(q_ref[0, :, cols], g_ref[0, :, cols], lane(columns, PAIR + a))


class Place:
    def __init__(self, start, heads, length, other_first, skipped=0):
        self.steps = heads // PAIR
        half = self.steps // 2
        base = start // PAIR
        width = PAIR * D

        def place(t, side):
            early = 1 - side[0] if other_first else side[0]
            return jnp.where(t < half, early * half + t, (1 - early) * half + t - half)

        skip = skipped // PAIR
        self.mine = pl.BlockSpec((PAIR, D, D), lambda t, s: (skip + jnp.minimum(t, half - 1), 0, 0))
        self.other = pl.BlockSpec((PAIR, D, D), lambda t, s: (skip + jnp.maximum(t - half, 0), 0, 0))
        self.state = pl.BlockSpec((PAIR, D, D), lambda t, s: (t, 0, 0))
        self.wide = pl.BlockSpec((1, length, width), lambda t, s: (0, 0, base + place(t, s)))
        self.chunk = pl.BlockSpec((1, length, width), lambda t, s: (0, 0, place(t, s)))
        self.flat = pl.BlockSpec((length, width), lambda t, s: (0, place(t, s)))
        self.square = pl.BlockSpec((1, 1, PAIR, D, D), lambda t, s: (0, 0, base + place(t, s), 0, 0))
        self.pack = pl.BlockSpec((1, PACK, length), lambda t, s: (base + place(t, s), 0, 0))
        self.whole = pl.BlockSpec((length, length), lambda t, s: (0, 0))


def call(kernel, name, place, side, args, specs, out_shapes, out_specs, kept, cost, limit=VMEM_BYTES):
    args = [side, *args]
    specs = list(specs)
    aliases = {}
    for n, value in enumerate(kept):
        if value is not None:
            aliases[len(args)] = n
            args.append(value)
            specs.append(pl.BlockSpec(memory_space=pl.ANY))
    return pl.pallas_call(
        kernel,
        out_shape=tuple(out_shapes),
        grid_spec=pltpu.PrefetchScalarGridSpec(
            num_scalar_prefetch=1, grid=(place.steps,), in_specs=specs, out_specs=list(out_specs)
        ),
        input_output_aliases=aliases,
        compiler_params=pltpu.CompilerParams(vmem_limit_bytes=limit),
        cost_estimate=pl.CostEstimate(**cost),
        name=name,
    )(*args)


def states_of(side, q, g, pack, start, heads):
    length = q.shape[1]
    at = Place(start, heads, length, True)
    state = jax.ShapeDtypeStruct((heads, D, D), jnp.float32)
    cost = dict(
        flops=heads * length * D * D * 2, bytes_accessed=heads * length * D * 26, transcendentals=0
    )
    return call(
        state_kernel,
        "head_states",
        at,
        side,
        (q, g, pack),
        (at.wide, at.chunk, at.pack),
        (state,),
        (at.state,),
        (),
        cost,
    )[0]


def inner_kernel(with_states, side_ref, q_ref, k_ref, v_ref, g_ref, p_ref, mask_ref, pack_ref, *rest):
    if with_states:
        gq_ref, gk_ref, gv_ref, state_ref = rest[-4:]
    else:
        gq_ref, gk_ref, gv_ref = rest[-3:]
    length = q_ref.shape[1]
    blocks = length // D
    columns = jnp.transpose(pack_ref[0])
    for a in range(PAIR):
        cols = slice(a * D, (a + 1) * D)
        q = q_ref[0, :, cols]
        k = k_ref[0, :, cols]
        v = v_ref[0, :, cols]
        g = g_ref[0, :, cols]
        head_weight = lane(columns, PAIR + a)
        if with_states:
            state_ref[a] = state_of(q, g, head_weight)
        row = pack_ref[0, a : a + 1, :]
        col = lane(columns, a)
        mixes = []
        for j in range(blocks):
            js = slice(j * D, (j + 1) * D)
            width = length - j * D
            late = slice(j * D, length)
            spread = row[:, late] - jnp.concatenate([col[js]] * (width // D), axis=1)
            weight = jnp.exp(spread + mask_ref[js, late])
            attention = (weight * dot(k[js], q[late], NT)).astype(jnp.bfloat16)
            mix = (weight * dot(v[js], g[late], NT)).astype(jnp.bfloat16)
            mixes.append(mix)
            gv_ref[js, cols] = dot(attention, g[late], NN)
            gk_ref[js, cols] = dot(mix, q[late], NN)
        prefix = dot(g, p_ref[0, 0, a].astype(jnp.bfloat16), NT) * head_weight
        for i in range(blocks):
            rows = slice(i * D, (i + 1) * D)
            parts = [mixes[j][:, (i - j) * D : (i - j + 1) * D] for j in range(i + 1)]
            mix = parts[0] if i == 0 else jnp.concatenate(parts, axis=0)
            gq = dot(mix, k[: (i + 1) * D], TN) + prefix[rows]
            gq_ref[0, rows, cols] = gq.astype(gq_ref.dtype)


def inner_of(side, q, k, v, g, prefix, mask, pack, out, start, heads, with_states):
    length = q.shape[1]
    at = Place(start, heads, length, True)
    partial = jax.ShapeDtypeStruct((length, heads * D), jnp.float32)
    state = jax.ShapeDtypeStruct((heads, D, D), jnp.float32)
    whole = jax.ShapeDtypeStruct(q.shape, jnp.bfloat16)
    cost = dict(
        flops=heads * 33 * 2 * D * D * D,
        bytes_accessed=heads * length * D * 80,
        transcendentals=heads * length * length // 2,
    )
    return call(
        functools.partial(inner_kernel, with_states),
        "inner_grads",
        at,
        side,
        (q, k, v, g, prefix, mask, pack),
        (at.wide, at.wide, at.wide, at.chunk, at.square, at.whole, at.pack),
        (whole, partial, partial) + ((state,) if with_states else ()),
        (at.wide, at.flat, at.flat) + ((at.state,) if with_states else ()),
        (out,),
        cost,
        VMEM_BYTES if start else 58 << 20,
    )


def finish_kernel(side_ref, k_ref, v_ref, ki_ref, vi_ref, mine_ref, other_ref, pack_ref, *rest):
    gk_ref, gv_ref = rest[-2:]
    first = pl.program_id(0) < pl.num_programs(0) // 2
    columns = jnp.transpose(pack_ref[0])
    for a in range(PAIR):
        cols = slice(a * D, (a + 1) * D)
        weight = lane(columns, 2 * PAIR + a)
        suffix = jnp.where(first, mine_ref[a], other_ref[a])
        gk = ki_ref[:, cols] + weight * dot(v_ref[0, :, cols], suffix, NT)
        gv = vi_ref[:, cols] + weight * dot(k_ref[0, :, cols], suffix, NN)
        gk_ref[0, :, cols] = gk.astype(gk_ref.dtype)
        gv_ref[0, :, cols] = gv.astype(gv_ref.dtype)


def finish_of(side, k, v, key_inner, value_inner, mine, other, pack, outs, start, heads, skipped):
    length = k.shape[1]
    at = Place(start, heads, length, False, skipped)
    whole = jax.ShapeDtypeStruct(k.shape, jnp.bfloat16)
    cost = dict(
        flops=heads * 6 * 2 * D * D * D, bytes_accessed=heads * length * D * 30, transcendentals=0
    )
    return call(
        finish_kernel,
        "finish_grads",
        at,
        side,
        (k, v, key_inner, value_inner, mine, other, pack),
        (at.wide, at.wide, at.flat, at.flat, at.mine, at.other, at.pack),
        (whole, whole),
        (at.wide, at.wide),
        outs,
        cost,
    )


def moved(value, pairs):
    return lax.ppermute(value, "ctx", pairs)


def part_of(table, first, count):
    return lax.dynamic_slice_in_dim(table, first, count)[:, None, None]


def after(value, *others):
    return lax.optimization_barrier((value, *others))[0]


def on_device(queries, key_rows, value_rows, next_grads, log_decay, doc_ids, prefix_states):
    pipe = lax.axis_size("pipe")
    ctx = lax.axis_size("ctx")
    length = queries.shape[1]
    back = [((i + 1) % pipe, i) for i in range(pipe)]
    core_swap = [(i, i ^ 1) for i in range(ctx)]
    chip_swap = [(i, i ^ 2) for i in range(ctx)]
    row_up = [[(i, i - 4 * d) for i in range(4 * d, ctx)] for d in (1, 2)]

    starts = [sum(CHUNKS[:n]) for n in range(len(CHUNKS))]
    docs = doc_ids[0]
    opening = lax.slice_in_dim(next_grads, 0, CHUNKS[0] * D, axis=2)
    grads = [lax.ppermute(opening, "pipe", back)]
    docs, log_decay = lax.optimization_barrier((docs, log_decay, opening))[:2]
    prior = lax.ppermute(docs[-1:] + 1, "ctx", [(i, i + 1) for i in range(ctx - 1)])[0]

    place = lax.axis_index("ctx")
    side = place % 2
    pair = (place // 2) % 2
    even = side == 0
    near = pair == 0
    continues = prior == docs[0] + 1
    position = lax.iota(jnp.int32, length)
    upto = jnp.where(position[:, None] <= position[None, :], 1.0, 0.0)
    running = jnp.dot(log_decay[0], upto, precision=lax.Precision.HIGHEST)
    allowed = (docs[:, None] == docs[None, :]) & (position[:, None] <= position[None, :])
    mask = jnp.where(allowed, 0.0, -1e30)
    total = running[:, -1:]
    head_weight = jnp.exp(running) * jnp.where((docs == docs[0]) & continues, 1.0, 0.0)
    tail_weight = jnp.exp(total - running) * jnp.where(docs == docs[-1], 1.0, 0.0)
    pack = jnp.concatenate(
        [
            value.reshape(-1, PAIR, length)
            for value in (running, head_weight, tail_weight, jnp.zeros_like(running))
        ],
        axis=1,
    )
    link = jnp.where((docs[0] == docs[-1]) & continues, jnp.exp(running[:, -1]), 0.0)
    side_arr = side.astype(jnp.int32).reshape(1)

    for start, size in list(zip(starts, CHUNKS))[1:]:
        part = lax.slice_in_dim(after(next_grads, running), start * D, (start + size) * D, axis=2)
        ready = part if len(grads) == 1 else after(part, grads[0])
        grads.append(lax.ppermute(ready, "pipe", back))

    def halves(table, members):
        return jnp.concatenate([part_of(table, starts[n] + side * (CHUNKS[n] // 2), CHUNKS[n] // 2) for n in members])

    held = []
    out = None
    members = []
    for group in GROUPS:
        begin = members[-1] + 1 if members else 0
        members = list(range(begin, begin + len(group)))
        inner = {}
        states = []
        late = None
        for n in members:
            start, size, grad = starts[n], CHUNKS[n], grads[n]
            if out is not None:
                grad = after(grad, out)
            if begin and n < len(CHUNKS) - 1:
                grad = after(grad, low)
            inputs = (prefix_states, mask, pack, out, start, size)
            if n == len(CHUNKS) - 1:
                state = states_of(side_arr, queries, grad, pack, start, size)
                late = (n, grad, inputs)
                before_last = out
            else:
                out, *inner[n], state = inner_of(side_arr, queries, key_rows, value_rows, grad, *inputs, True)
            states.append(state)
            if n == 0:
                first_out = out
        if begin == 0:
            link = after(link, first_out)
            partner = moved(link, core_swap)
            link_even = jnp.where(even, link, partner)
            link_odd = jnp.where(even, partner, link)
            chip_link = link_even * link_odd
            near_table = jnp.stack([chip_link] + [moved(chip_link, pairs) for pairs in row_up])
        other = jnp.concatenate([state[: state.shape[0] // 2] for state in states])
        mine = jnp.concatenate([state[state.shape[0] // 2 :] for state in states])
        came = moved(other, core_swap)
        if begin:
            came = after(came, *held[-1][3])
        even_state = jnp.where(even, mine, came)
        odd_state = jnp.where(even, came, mine)
        state = even_state + halves(link_even, members) * odd_state
        low = state.astype(jnp.bfloat16)
        later = [moved(low, pairs) for pairs in row_up]
        if late is not None:
            n, grad, inputs = late
            out, *inner[n] = inner_of(side_arr, queries, key_rows, value_rows, after(grad, low), *inputs, False)
        held.append((members, odd_state, state, later, inner))

    beside = after(moved(near_table, chip_swap), before_last)
    near_rows = jnp.where(near, near_table, beside)
    far_rows = jnp.where(near, beside, near_table)
    far_link, next_near, next_far, last_near = far_rows[0], near_rows[1], far_rows[1], near_rows[2]
    own_coef = [
        jnp.where(near, far_link, next_near),
        jnp.where(near, far_link * next_near * next_far, next_near * next_far * last_near),
    ]
    sent_coef = jnp.where(near, next_near * next_far, far_link * next_near)
    outs = (None, None)
    for members, odd_state, state, later, inner in held:
        state = after(state, out if members[-1] == len(CHUNKS) - 1 else grads[-1])
        later = [value.astype(jnp.float32) for value in later]
        near_coef, far_coef = (halves(table, members) for table in own_coef)
        coef = halves(sent_coef, members)
        sent = jnp.where(near, later[0] + coef * later[1], state + coef * later[0])
        came = moved(sent.astype(jnp.bfloat16), chip_swap)
        came = after(came, out) if outs[0] is None else after(came, *first_outs)
        came = came.astype(jnp.float32)
        suffix = near_coef * later[0] + far_coef * later[1] + came
        within = odd_state + halves(link_odd, members) * suffix
        mine_suffix = jnp.where(even, within, suffix).astype(jnp.bfloat16)
        send_suffix = jnp.where(even, suffix, within).astype(jnp.bfloat16)
        other_suffix = moved(send_suffix, core_swap)
        skipped = 0
        for n in members:
            outs = finish_of(
                side_arr,
                key_rows,
                value_rows,
                *inner[n],
                mine_suffix,
                other_suffix,
                pack,
                outs,
                starts[n],
                CHUNKS[n],
                skipped,
            )
            skipped += CHUNKS[n] // 2
            if n == 0:
                first_outs = outs
    return (out, *outs)


def solution(mesh):
    rows = P("pipe", "ctx", None)
    return jax.shard_map(
        on_device,
        mesh=mesh,
        in_specs=(
            rows,
            rows,
            rows,
            rows,
            P("pipe", None, "ctx"),
            P("pipe", "ctx"),
            P("pipe", "ctx", None, None, None),
        ),
        out_specs=(rows, rows, rows),
        check_vma=False,
    )
```

```python
import functools

import jax
import jax.numpy as jnp
from jax import lax
from jax.experimental import pallas as pl
from jax.experimental.pallas import tpu as pltpu
from jax.sharding import PartitionSpec as P

D = 128
GROUPS = ((8, 12), (8, 4))
CHUNKS = sum(GROUPS, ())
PAIR = 2
PACK = 8
VMEM_BYTES = 36 << 20
NT = (((1,), (1,)), ((), ()))
NN = (((1,), (0,)), ((), ()))
TN = (((0,), (0,)), ((), ()))


def dot(a, b, dims):
    return lax.dot_general(a, b, dims, preferred_element_type=jnp.float32)


def lane(columns, n):
    return jnp.broadcast_to(columns[:, n : n + 1], (columns.shape[0], D))


def state_of(q, g, head_weight):
    weighted = (head_weight * g.astype(jnp.float32)).astype(jnp.bfloat16)
    return dot(q, weighted, TN)


def state_kernel(side_ref, q_ref, g_ref, pack_ref, state_ref):
    columns = jnp.transpose(pack_ref[0])
    for a in range(PAIR):
        cols = slice(a * D, (a + 1) * D)
        state_ref[a] = state_of(q_ref[0, :, cols], g_ref[0, :, cols], lane(columns, PAIR + a))


class Place:
    def __init__(self, start, heads, length, other_first, skipped=0):
        self.steps = heads // PAIR
        half = self.steps // 2
        base = start // PAIR
        width = PAIR * D

        def place(t, side):
            early = 1 - side[0] if other_first else side[0]
            return jnp.where(t < half, early * half + t, (1 - early) * half + t - half)

        skip = skipped // PAIR
        self.mine = pl.BlockSpec((PAIR, D, D), lambda t, s: (skip + jnp.minimum(t, half - 1), 0, 0))
        self.other = pl.BlockSpec((PAIR, D, D), lambda t, s: (skip + jnp.maximum(t - half, 0), 0, 0))
        self.state = pl.BlockSpec((PAIR, D, D), lambda t, s: (t, 0, 0))
        self.wide = pl.BlockSpec((1, length, width), lambda t, s: (0, 0, base + place(t, s)))
        self.chunk = pl.BlockSpec((1, length, width), lambda t, s: (0, 0, place(t, s)))
        self.flat = pl.BlockSpec((length, width), lambda t, s: (0, place(t, s)))
        self.square = pl.BlockSpec((1, 1, PAIR, D, D), lambda t, s: (0, 0, base + place(t, s), 0, 0))
        self.pack = pl.BlockSpec((1, PACK, length), lambda t, s: (base + place(t, s), 0, 0))
        self.whole = pl.BlockSpec((length, length), lambda t, s: (0, 0))


def call(kernel, name, place, side, args, specs, out_shapes, out_specs, kept, cost, limit=VMEM_BYTES):
    args = [side, *args]
    specs = list(specs)
    aliases = {}
    for n, value in enumerate(kept):
        if value is not None:
            aliases[len(args)] = n
            args.append(value)
            specs.append(pl.BlockSpec(memory_space=pl.ANY))
    return pl.pallas_call(
        kernel,
        out_shape=tuple(out_shapes),
        grid_spec=pltpu.PrefetchScalarGridSpec(
            num_scalar_prefetch=1, grid=(place.steps,), in_specs=specs, out_specs=list(out_specs)
        ),
        input_output_aliases=aliases,
        compiler_params=pltpu.CompilerParams(vmem_limit_bytes=limit),
        cost_estimate=pl.CostEstimate(**cost),
        name=name,
    )(*args)


def states_of(side, q, g, pack, start, heads):
    length = q.shape[1]
    at = Place(start, heads, length, True)
    state = jax.ShapeDtypeStruct((heads, D, D), jnp.float32)
    cost = dict(
        flops=heads * length * D * D * 2, bytes_accessed=heads * length * D * 26, transcendentals=0
    )
    return call(
        state_kernel,
        "head_states",
        at,
        side,
        (q, g, pack),
        (at.wide, at.chunk, at.pack),
        (state,),
        (at.state,),
        (),
        cost,
    )[0]


def inner_kernel(with_states, side_ref, q_ref, k_ref, v_ref, g_ref, p_ref, mask_ref, pack_ref, *rest):
    if with_states:
        gq_ref, gk_ref, gv_ref, state_ref = rest[-4:]
    else:
        gq_ref, gk_ref, gv_ref = rest[-3:]
    length = q_ref.shape[1]
    blocks = length // D
    columns = jnp.transpose(pack_ref[0])
    for a in range(PAIR):
        cols = slice(a * D, (a + 1) * D)
        q = q_ref[0, :, cols]
        k = k_ref[0, :, cols]
        v = v_ref[0, :, cols]
        g = g_ref[0, :, cols]
        head_weight = lane(columns, PAIR + a)
        if with_states:
            state_ref[a] = state_of(q, g, head_weight)
        row = pack_ref[0, a : a + 1, :]
        col = lane(columns, a)
        mixes = []
        for j in range(blocks):
            js = slice(j * D, (j + 1) * D)
            width = length - j * D
            late = slice(j * D, length)
            spread = row[:, late] - jnp.concatenate([col[js]] * (width // D), axis=1)
            weight = jnp.exp(spread + mask_ref[js, late])
            attention = (weight * dot(k[js], q[late], NT)).astype(jnp.bfloat16)
            mix = (weight * dot(v[js], g[late], NT)).astype(jnp.bfloat16)
            mixes.append(mix)
            gv_ref[js, cols] = dot(attention, g[late], NN)
            gk_ref[js, cols] = dot(mix, q[late], NN)
        prefix = dot(g, p_ref[0, 0, a].astype(jnp.bfloat16), NT) * head_weight
        for i in range(blocks):
            rows = slice(i * D, (i + 1) * D)
            parts = [mixes[j][:, (i - j) * D : (i - j + 1) * D] for j in range(i + 1)]
            mix = parts[0] if i == 0 else jnp.concatenate(parts, axis=0)
            gq = dot(mix, k[: (i + 1) * D], TN) + prefix[rows]
            gq_ref[0, rows, cols] = gq.astype(gq_ref.dtype)


def inner_of(side, q, k, v, g, prefix, mask, pack, out, start, heads, with_states):
    length = q.shape[1]
    at = Place(start, heads, length, True)
    partial = jax.ShapeDtypeStruct((length, heads * D), jnp.float32)
    state = jax.ShapeDtypeStruct((heads, D, D), jnp.float32)
    whole = jax.ShapeDtypeStruct(q.shape, jnp.bfloat16)
    cost = dict(
        flops=heads * 33 * 2 * D * D * D,
        bytes_accessed=heads * length * D * 80,
        transcendentals=heads * length * length // 2,
    )
    return call(
        functools.partial(inner_kernel, with_states),
        "inner_grads",
        at,
        side,
        (q, k, v, g, prefix, mask, pack),
        (at.wide, at.wide, at.wide, at.chunk, at.square, at.whole, at.pack),
        (whole, partial, partial) + ((state,) if with_states else ()),
        (at.wide, at.flat, at.flat) + ((at.state,) if with_states else ()),
        (out,),
        cost,
        VMEM_BYTES if start else 58 << 20,
    )


def finish_kernel(side_ref, k_ref, v_ref, ki_ref, vi_ref, mine_ref, other_ref, pack_ref, *rest):
    gk_ref, gv_ref = rest[-2:]
    first = pl.program_id(0) < pl.num_programs(0) // 2
    columns = jnp.transpose(pack_ref[0])
    for a in range(PAIR):
        cols = slice(a * D, (a + 1) * D)
        weight = lane(columns, 2 * PAIR + a)
        suffix = jnp.where(first, mine_ref[a], other_ref[a])
        gk = ki_ref[:, cols] + weight * dot(v_ref[0, :, cols], suffix, NT)
        gv = vi_ref[:, cols] + weight * dot(k_ref[0, :, cols], suffix, NN)
        gk_ref[0, :, cols] = gk.astype(gk_ref.dtype)
        gv_ref[0, :, cols] = gv.astype(gv_ref.dtype)


def finish_of(side, k, v, key_inner, value_inner, mine, other, pack, outs, start, heads, skipped):
    length = k.shape[1]
    at = Place(start, heads, length, False, skipped)
    whole = jax.ShapeDtypeStruct(k.shape, jnp.bfloat16)
    cost = dict(
        flops=heads * 6 * 2 * D * D * D, bytes_accessed=heads * length * D * 30, transcendentals=0
    )
    return call(
        finish_kernel,
        "finish_grads",
        at,
        side,
        (k, v, key_inner, value_inner, mine, other, pack),
        (at.wide, at.wide, at.flat, at.flat, at.mine, at.other, at.pack),
        (whole, whole),
        (at.wide, at.wide),
        outs,
        cost,
    )


def moved(value, pairs):
    return lax.ppermute(value, "ctx", pairs)


def part_of(table, first, count):
    return lax.dynamic_slice_in_dim(table, first, count)[:, None, None]


def after(value, *others):
    return lax.optimization_barrier((value, *others))[0]


def on_device(queries, key_rows, value_rows, next_grads, log_decay, doc_ids, prefix_states):
    pipe = lax.axis_size("pipe")
    ctx = lax.axis_size("ctx")
    length = queries.shape[1]
    back = [((i + 1) % pipe, i) for i in range(pipe)]
    core_swap = [(i, i ^ 1) for i in range(ctx)]
    chip_swap = [(i, i ^ 2) for i in range(ctx)]
    row_up = [[(i, i - 4 * d) for i in range(4 * d, ctx)] for d in (1, 2)]

    starts = [sum(CHUNKS[:n]) for n in range(len(CHUNKS))]
    docs = doc_ids[0]
    opening = lax.slice_in_dim(next_grads, 0, CHUNKS[0] * D, axis=2)
    grads = [lax.ppermute(opening, "pipe", back)]
    docs, log_decay = lax.optimization_barrier((docs, log_decay, opening))[:2]
    prior = lax.ppermute(docs[-1:] + 1, "ctx", [(i, i + 1) for i in range(ctx - 1)])[0]

    place = lax.axis_index("ctx")
    side = place % 2
    pair = (place // 2) % 2
    even = side == 0
    near = pair == 0
    continues = prior == docs[0] + 1
    position = lax.iota(jnp.int32, length)
    upto = jnp.where(position[:, None] <= position[None, :], 1.0, 0.0)
    running = jnp.dot(log_decay[0], upto, precision=lax.Precision.HIGHEST)
    allowed = (docs[:, None] == docs[None, :]) & (position[:, None] <= position[None, :])
    mask = jnp.where(allowed, 0.0, -1e30)
    total = running[:, -1:]
    head_weight = jnp.exp(running) * jnp.where((docs == docs[0]) & continues, 1.0, 0.0)
    tail_weight = jnp.exp(total - running) * jnp.where(docs == docs[-1], 1.0, 0.0)
    pack = jnp.concatenate(
        [
            value.reshape(-1, PAIR, length)
            for value in (running, head_weight, tail_weight, jnp.zeros_like(running))
        ],
        axis=1,
    )
    link = jnp.where((docs[0] == docs[-1]) & continues, jnp.exp(running[:, -1]), 0.0)
    side_arr = side.astype(jnp.int32).reshape(1)

    for start, size in list(zip(starts, CHUNKS))[1:]:
        part = lax.slice_in_dim(after(next_grads, running), start * D, (start + size) * D, axis=2)
        ready = part if len(grads) == 1 else after(part, grads[len(grads) - 2])
        grads.append(lax.ppermute(ready, "pipe", back))

    def halves(table, members):
        return jnp.concatenate([part_of(table, starts[n] + side * (CHUNKS[n] // 2), CHUNKS[n] // 2) for n in members])

    held = []
    out = None
    members = []
    for group in GROUPS:
        begin = members[-1] + 1 if members else 0
        members = list(range(begin, begin + len(group)))
        inner = {}
        states = []
        late = None
        for n in members:
            start, size, grad = starts[n], CHUNKS[n], grads[n]
            if out is not None:
                grad = after(grad, out)
            if begin and n < len(CHUNKS) - 1:
                grad = after(grad, low)
            inputs = (prefix_states, mask, pack, out, start, size)
            if n == len(CHUNKS) - 1:
                state = states_of(side_arr, queries, grad, pack, start, size)
                late = (n, grad, inputs)
                before_last = out
            else:
                out, *inner[n], state = inner_of(side_arr, queries, key_rows, value_rows, grad, *inputs, True)
            states.append(state)
            if n == 0:
                first_out = out
        if begin == 0:
            link = after(link, first_out)
            partner = moved(link, core_swap)
            link_even = jnp.where(even, link, partner)
            link_odd = jnp.where(even, partner, link)
            chip_link = link_even * link_odd
            near_table = jnp.stack([chip_link] + [moved(chip_link, pairs) for pairs in row_up])
        other = jnp.concatenate([state[: state.shape[0] // 2] for state in states])
        mine = jnp.concatenate([state[state.shape[0] // 2 :] for state in states])
        came = moved(other, core_swap)
        if begin:
            came = after(came, *held[-1][3])
        even_state = jnp.where(even, mine, came)
        odd_state = jnp.where(even, came, mine)
        state = even_state + halves(link_even, members) * odd_state
        low = state.astype(jnp.bfloat16)
        later = [moved(low, pairs) for pairs in row_up]
        if late is not None:
            n, grad, inputs = late
            out, *inner[n] = inner_of(side_arr, queries, key_rows, value_rows, after(grad, low), *inputs, False)
        held.append((members, odd_state, state, later, inner))

    beside = after(moved(near_table, chip_swap), before_last)
    near_rows = jnp.where(near, near_table, beside)
    far_rows = jnp.where(near, beside, near_table)
    far_link, next_near, next_far, last_near = far_rows[0], near_rows[1], far_rows[1], near_rows[2]
    own_coef = [
        jnp.where(near, far_link, next_near),
        jnp.where(near, far_link * next_near * next_far, next_near * next_far * last_near),
    ]
    sent_coef = jnp.where(near, next_near * next_far, far_link * next_near)
    outs = (None, None)
    for members, odd_state, state, later, inner in held:
        state = after(state, out if members[-1] == len(CHUNKS) - 1 else grads[-1])
        later = [value.astype(jnp.float32) for value in later]
        near_coef, far_coef = (halves(table, members) for table in own_coef)
        coef = halves(sent_coef, members)
        sent = jnp.where(near, later[0] + coef * later[1], state + coef * later[0])
        came = moved(sent.astype(jnp.bfloat16), chip_swap)
        came = after(came, out) if outs[0] is None else after(came, *first_outs)
        came = came.astype(jnp.float32)
        suffix = near_coef * later[0] + far_coef * later[1] + came
        within = odd_state + halves(link_odd, members) * suffix
        mine_suffix = jnp.where(even, within, suffix).astype(jnp.bfloat16)
        send_suffix = jnp.where(even, suffix, within).astype(jnp.bfloat16)
        other_suffix = moved(send_suffix, core_swap)
        skipped = 0
        for n in members:
            outs = finish_of(
                side_arr,
                key_rows,
                value_rows,
                *inner[n],
                mine_suffix,
                other_suffix,
                pack,
                outs,
                starts[n],
                CHUNKS[n],
                skipped,
            )
            skipped += CHUNKS[n] // 2
            if n == 0:
                first_outs = outs
    return (out, *outs)


def solution(mesh):
    rows = P("pipe", "ctx", None)
    return jax.shard_map(
        on_device,
        mesh=mesh,
        in_specs=(
            rows,
            rows,
            rows,
            rows,
            P("pipe", None, "ctx"),
            P("pipe", "ctx"),
            P("pipe", "ctx", None, None, None),
        ),
        out_specs=(rows, rows, rows),
        check_vma=False,
    )
```
